512 devices in a mesh: row: 32 (over y, x_hi, core), col: 16 (over x_lo, z).
Axes of the slice: x: 4 (x_hi: 2, x_lo: 2; x = x_hi * 2 + x_lo), y: 8, z: 8, core: 2. Of those that a mesh axis runs over, the one named last changes fastest.
Arguments:
- perturbation: bfloat16 [16384, 16384], P('row', 'col'), may hold values from -0.046875 to 0.046875
- basis: bfloat16 [16384, 16384], P('row', 'col'), may hold values from -0.125 to 0.125
- orbitals: bfloat16 [16384, 512], P('col', 'row'), may hold values from -6 to 6
- pair_mask: int32 [16384, 512], P('col'), may hold values 0 or 1
- energies: float32 [16384], P('col'), may hold values from 1 to 4
- occ_energies: float32 [512], replicated, may hold values from -3 to -1
Outputs:
- response: float32 [16384, 512], P('row', 'col')
The draws below stay inside these ranges and needn't reach their ends.
All inputs are finite; a program needn't handle non-finite values. No bound on the sum of `pair_mask` on one device may be relied on, other than what follows from the above.
Results may differ from the reference program's by a relative error of at most 0.0037.
Values may be sent and summed in bfloat16 or wider, within the bound.
No kernel may reach another device: no remote copies, remote signals or barrier semaphores. Data moves between devices by JAX's collectives and lax.ppermute only.
A program may use at most 64 MiB of HBM per device.

```python
import jax
import jax.numpy as jnp

M = 16384
NOCC = 512


def touch_ends(array, rng, least, top_value):
    place = [jax.random.randint(jax.random.fold_in(rng, axis), (), 0, length) for axis, length in enumerate(array.shape)]
    main_axis = array.shape.index(max(array.shape))
    next_to = place[:main_axis] + [(place[main_axis] + 1) % array.shape[main_axis]] + place[main_axis + 1:]
    return array.at[tuple(place)].set(least).at[tuple(next_to)].set(top_value)


def steps_of(rng, dims, cuts, low, high):
    factor_of, own = 1.0, jax.random.fold_in(rng, 6)
    for axis_at, blocks in cuts:
        heights = jnp.exp(jax.random.uniform(jax.random.fold_in(own, axis_at), (blocks,), jnp.float32, low / len(cuts), high / len(cuts)))
        factor_of = factor_of * jnp.repeat(heights, dims[axis_at] // blocks).reshape([-1 if axis == axis_at else 1 for axis in range(len(dims))])
    return factor_of


def noise(rng, shape, spread, bound, pieces=(), dtype=jnp.bfloat16):
    gain = steps_of(rng, shape, pieces, -0.22, 0.18) if pieces else 1.0
    result = jax.random.normal(rng, shape, jnp.float32) * spread * gain
    return jnp.minimum(jnp.maximum(result, -bound), bound).astype(dtype)


def setup_inputs(seed: int = 0) -> dict:
    arg_keys = jax.random.split(jax.random.key(seed), 7)
    perturbation = noise(arg_keys[0], (M, M), M ** -0.5, 0.046875, ((0, 32), (1, 16)))
    basis = noise(arg_keys[1], (M, M), (M // 8) ** -0.5, 0.125, ((0, 32), (1, 16)))
    orbitals = noise(arg_keys[2], (M, NOCC), 1.0, 6.0, ((0, 16), (1, 32)))
    pair_mask = touch_ends((jax.random.randint(arg_keys[3], (M, NOCC), 0, 4) < 3).astype(jnp.int32), jax.random.fold_in(arg_keys[3], 1), 0, 1)
    energies = jnp.clip(1.0 + 3.0 * jax.random.uniform(arg_keys[4], (M,), jnp.float32) ** steps_of(arg_keys[4], (M,), ((0, 16),), -0.2, 0.2), 1.0, 4.0)
    occ_energies = jnp.clip(jax.random.uniform(arg_keys[5], (NOCC,), jnp.float32, -3.0, -1.0), -3.0, -1.0)
    return dict(perturbation=perturbation, basis=basis, orbitals=orbitals, pair_mask=pair_mask, energies=energies, occ_energies=occ_energies)


def reference(perturbation, basis, orbitals, pair_mask, energies, occ_energies):
    image = jnp.dot(perturbation, orbitals, preferred_element_type=jnp.float32).astype(jnp.bfloat16)
    projection = jnp.dot(basis.T, image, preferred_element_type=jnp.float32)
    spacing = energies[:, None] - occ_energies[None, :]
    coefficients = jnp.where(pair_mask == 1, projection / spacing, jnp.zeros_like(projection)).astype(jnp.bfloat16)
    return jnp.dot(basis, coefficients, preferred_element_type=jnp.float32)
```

```python
import jax
import jax.numpy as jnp
from jax import lax
from jax.sharding import Mesh, PartitionSpec as P

ROW = ("y", "xh")
COL = ("xl", "z")
BF16, F32 = jnp.bfloat16, jnp.float32


def exchange(pieces, axes):
    return lax.all_to_all(pieces, axes, 0, 0)


def spread(piece, axes):
    count = lax.axis_size(axes)
    got = exchange(jnp.broadcast_to(piece[None], (count,) + piece.shape), axes)
    return got.reshape((count * piece.shape[0],) + piece.shape[1:])


def collect(part, axes, dtype):
    count = lax.axis_size(axes)
    pieces = part.astype(dtype).reshape((count, part.shape[0] // count) + part.shape[1:])
    return exchange(pieces, axes).astype(F32).sum(axis=0)


def dot_nt(a, b):
    return lax.dot_general(a, b, (((1,), (1,)), ((), ())), preferred_element_type=F32)


def dot_nn(a, b):
    return lax.dot_general(a, b, (((1,), (0,)), ((), ())), preferred_element_type=F32)


def shards(perturbation, basis, orbitals, pair_mask, energies, occ_energies):
    swap = [(0, 1), (1, 0)]
    core = lax.axis_index("core")
    width = orbitals.shape[1]
    rows = perturbation.shape[0]
    pert_other = lax.ppermute(perturbation, "core", swap)
    basis_other = lax.ppermute(basis, "core", swap)

    first = lax.axis_index(ROW + ("core",)) * width
    mask_t = lax.dynamic_slice_in_dim(pair_mask, first, width, 1).T
    occ = lax.dynamic_slice_in_dim(occ_energies, first, width, 0)
    weight = jnp.where(mask_t == 1, 1.0 / (energies[None, :] - occ[:, None]), 0.0)

    orbs = spread(orbitals.T, ROW)
    part = jnp.concatenate([dot_nt(orbs, perturbation), dot_nt(orbs, pert_other)], axis=1)
    image = spread(collect(part, COL, F32).astype(BF16), COL)
    part = dot_nn(image[:, :rows], basis) + dot_nn(image[:, rows:], basis_other)
    coef = spread((collect(part, ROW, BF16) * weight).astype(BF16), ROW)
    part = jnp.concatenate([dot_nt(coef, basis), dot_nt(coef, basis_other)], axis=1)
    mine = collect(part, COL, BF16)
    keep, give = mine[:, :rows], mine[:, rows:]
    got = lax.ppermute(give, "core", swap)
    out = jnp.concatenate(
        [jnp.where(core == 0, keep, got), jnp.where(core == 0, got, keep)], axis=0
    )
    return out.T


def solution(mesh):
    sizes = (mesh.shape["row"] // 4, 2, 2, 2, mesh.shape["col"] // 2)
    fine = Mesh(mesh.devices.reshape(sizes), ("y", "xh", "core", "xl", "z"))
    row, col = ("y", "xh", "core"), ("xl", "z")
    return jax.shard_map(
        shards,
        mesh=fine,
        in_specs=(P(row, col), P(row, col), P(col, row), P(col, None), P(col), P()),
        out_specs=P(row, col),
        check_vma=False,
    )
```

```python
import jax
import jax.numpy as jnp
from jax import lax
from jax.experimental import pallas as pl
from jax.experimental.pallas import tpu as pltpu
from jax.sharding import Mesh, PartitionSpec as P


ROW = ("y", "xh")
COL = ("xl", "z")
BF16, F32 = jnp.bfloat16, jnp.float32
NT = (((1,), (1,)), ((), ()))
NN = (((1,), (0,)), ((), ()))


def exchange(pieces, axes):
    return lax.all_to_all(pieces, axes, 0, 0)


def local(kernel, out, *operands):
    one = not isinstance(out, list)
    outs = [jax.ShapeDtypeStruct(*o) for o in ([out] if one else out)]
    vmem = pl.BlockSpec(memory_space=pltpu.VMEM)
    got = pl.pallas_call(
        kernel,
        out_shape=outs,
        in_specs=[vmem if o.ndim > 1 else pl.BlockSpec(memory_space=pltpu.SMEM) for o in operands],
        out_specs=[vmem for _ in outs],
        compiler_params=pltpu.CompilerParams(vmem_limit_bytes=24 * 2**20),
        cost_estimate=pl.CostEstimate(
            flops=2048 * operands[0].size,
            transcendentals=0,
            bytes_accessed=sum(o.nbytes for o in operands),
        ),
    )(*operands)
    return got[0] if one else got


def total(ref):
    acc = ref[0].astype(F32)
    for k in range(1, ref.shape[0]):
        acc += ref[k].astype(F32)
    return acc


def stream_kernel(left_hbm, own_hbm, other_hbm, out_ref, left_ref, pert_ref, sem):
    rows, cols = own_hbm.shape
    cut = rows // 2
    copies = [pltpu.make_async_copy(left_hbm, left_ref, sem.at[4])]
    for k in range(4):
        src = (own_hbm, other_hbm)[k // 2].at[pl.ds(k % 2 * cut, cut)]
        copies.append(pltpu.make_async_copy(src, pert_ref.at[k], sem.at[k]))
    for copy in copies:
        copy.start()
    copies[0].wait()
    left = left_ref[...].reshape(-1, cols)
    for k in range(4):
        copies[1 + k].wait()
        part = lax.dot_general(left, pert_ref[k], NT, preferred_element_type=F32)
        out_ref[:, :, k * cut : (k + 1) * cut] = part.astype(BF16).reshape(
            out_ref.shape[0], out_ref.shape[1], cut
        )


def image_kernel(left_ref, own_ref, other_ref, out_ref):
    left = left_ref[...].reshape(-1, left_ref.shape[-1])
    rows = own_ref.shape[0]
    for k, ref in enumerate((own_ref, other_ref)):
        part = lax.dot_general(left, ref[...], NT, preferred_element_type=F32)
        out_ref[:, :, k * rows : (k + 1) * rows] = part.astype(BF16).reshape(
            out_ref.shape[0], out_ref.shape[1], rows
        )


def projection_kernel(left_ref, own_ref, other_ref, out_ref):
    rows = own_ref.shape[0]
    left = left_ref[...].reshape(-1, left_ref.shape[-1])
    part = lax.dot_general(left[:, :rows], own_ref[...], NN, preferred_element_type=F32)
    part += lax.dot_general(left[:, rows:], other_ref[...], NN, preferred_element_type=F32)
    out_ref[...] = part.astype(BF16).reshape(out_ref.shape)


def sum_kernel(got_ref, out_ref):
    out_ref[...] = jnp.broadcast_to(total(got_ref).astype(BF16)[None], out_ref.shape)


def scale_kernel(got_ref, weight_ref, out_ref):
    coef = (total(got_ref) * weight_ref[...]).astype(BF16)
    out_ref[...] = jnp.broadcast_to(coef[None], out_ref.shape)


def final_kernel(got_ref, own_ref, other_ref):
    rows = own_ref.shape[1]
    acc = total(got_ref)
    own_ref[...] = acc[:, :rows]
    other_ref[...] = acc[:, rows:]


def place_kernel(core_ref, own_ref, got_ref, out_ref):
    width = own_ref.shape[0]
    flip = core_ref[0] == 1
    own, got = own_ref[...], got_ref[...]
    out_ref[:width] = jnp.where(flip, got, own)
    out_ref[width:] = jnp.where(flip, own, got)


def steps(perturbation, basis, orbitals, pair_mask, energies, occ_energies):
    swap = [(0, 1), (1, 0)]
    core = lax.axis_index("core")
    rows, cols = perturbation.shape
    width = orbitals.shape[1]
    n_row, n_col = lax.axis_size(ROW), lax.axis_size(COL)
    share = width * n_row // n_col
    pert_other = lax.ppermute(perturbation, "core", swap)
    basis_other = lax.ppermute(basis, "core", swap)
    first = lax.axis_index(ROW + ("core",)) * width
    mask_t = lax.dynamic_slice_in_dim(pair_mask, first, width, 1).T
    occ = lax.dynamic_slice_in_dim(occ_energies, first, width, 0)
    weight = jnp.where(mask_t == 1, 1.0 / (energies[None, :] - occ[:, None]), 0.0)

    orbs = exchange(jnp.broadcast_to(orbitals.T[None], (n_row, width, cols)), ROW)
    orbs, pert_other, basis_other, weight = lax.optimization_barrier(
        (orbs, pert_other, basis_other, weight)
    )
    by_col, by_row = ((n_col, share, 2 * rows), BF16), ((n_row, width, cols), BF16)
    hbm = pl.BlockSpec(memory_space=pltpu.MemorySpace.HBM)
    part = pl.pallas_call(
        stream_kernel,
        out_shape=jax.ShapeDtypeStruct(*by_col),
        in_specs=[hbm] * 3,
        out_specs=pl.BlockSpec(memory_space=pltpu.VMEM),
        scratch_shapes=[
            pltpu.VMEM(orbs.shape, BF16),
            pltpu.VMEM((4, rows // 2, cols), BF16),
            pltpu.SemaphoreType.DMA((5,)),
        ],
        compiler_params=pltpu.CompilerParams(vmem_limit_bytes=24 * 2**20),
        cost_estimate=pl.CostEstimate(
            flops=4 * orbs.size * rows, transcendentals=0, bytes_accessed=3 * orbs.nbytes
        ),
        name="image",
    )(orbs, perturbation, pert_other)
    part = exchange(part, COL)
    image = exchange(local(sum_kernel, by_col, part), COL)
    part = exchange(local(projection_kernel, by_row, image, basis, basis_other), ROW)
    coef = exchange(local(scale_kernel, by_row, part, weight), ROW)
    part = exchange(local(image_kernel, by_col, coef, basis, basis_other), COL)
    own, other = local(final_kernel, [((share, rows), F32)] * 2, part)
    got = lax.ppermute(other, "core", swap)
    return local(place_kernel, ((2 * share, rows), F32), core.reshape(1), own, got).T


def solution(mesh):
    sizes = (mesh.shape["row"] // 4, 2, 2, 2, mesh.shape["col"] // 2)
    fine = Mesh(mesh.devices.reshape(sizes), ("y", "xh", "core", "xl", "z"))
    row, col = ("y", "xh", "core"), ("xl", "z")
    return jax.shard_map(
        steps,
        mesh=fine,
        in_specs=(P(row, col), P(row, col), P(col, row), P(col, None), P(col), P()),
        out_specs=P(row, col),
        check_vma=False,
    )
```

```python
import jax
import jax.numpy as jnp
from jax import lax
from jax.experimental import pallas as pl
from jax.experimental.pallas import tpu as pltpu
from jax.sharding import Mesh, PartitionSpec as P


ROW = ("y", "xh")
COL = ("xl", "z")
BF16, F32 = jnp.bfloat16, jnp.float32
NT = (((1,), (1,)), ((), ()))
NN = (((1,), (0,)), ((), ()))


def exchange(pieces, axes):
    return lax.all_to_all(pieces, axes, 0, 0)


def local(kernel, outs, *operands, scratch=(), hbm=()):
    places = [
        pltpu.SMEM if o.ndim == 1 else pl.ANY if k in hbm else pltpu.VMEM
        for k, o in enumerate(operands)
    ]
    return pl.pallas_call(
        kernel,
        out_shape=[jax.ShapeDtypeStruct(*o) for o in outs],
        in_specs=[pl.BlockSpec(memory_space=p) for p in places],
        out_specs=[pl.BlockSpec(memory_space=pltpu.VMEM) for _ in outs],
        scratch_shapes=list(scratch),
        compiler_params=pltpu.CompilerParams(vmem_limit_bytes=24 * 2**20),
        cost_estimate=pl.CostEstimate(
            flops=2**29, transcendentals=0, bytes_accessed=sum(o.nbytes for o in operands)
        ),
    )(*operands)


def put(part, lo, out_ref, acc_ref):
    cols = slice(lo, lo + part.shape[1])
    out_ref[:, :, cols] = part.astype(BF16).reshape(*out_ref.shape[:2], part.shape[1])
    acc_ref[:, cols] = part


def finish(at_ref, fix_ref, acc_ref):
    width = fix_ref.shape[0]
    kept = acc_ref[pl.ds(pl.multiple_of(at_ref[0] * width, width), width), :]
    fix_ref[...] = kept - kept.astype(BF16).astype(F32)


def total(got_ref, fix_ref):
    acc = fix_ref[...]
    for k in range(got_ref.shape[0]):
        acc += got_ref[k].astype(F32)
    return acc


def image_kernel(at_ref, left_ref, own_ref, other_hbm, out_ref, fix_ref, acc_ref, other_ref, sem):
    rows, cols = own_ref.shape
    cut = rows // 2
    copies = [
        pltpu.make_async_copy(other_hbm.at[pl.ds(k * cut, cut)], other_ref.at[k], sem.at[k])
        for k in range(2)
    ]
    for copy in copies:
        copy.start()
    left = left_ref[...].reshape(-1, cols)
    put(lax.dot_general(left, own_ref[...], NT, preferred_element_type=F32), 0, out_ref, acc_ref)
    for k in range(2):
        copies[k].wait()
        part = lax.dot_general(left, other_ref[k], NT, preferred_element_type=F32)
        put(part, rows + k * cut, out_ref, acc_ref)
    finish(at_ref, fix_ref, acc_ref)


def projection_kernel(at_ref, left_ref, own_ref, other_ref, out_ref, fix_ref, acc_ref):
    rows = own_ref.shape[0]
    left = left_ref[...].reshape(-1, left_ref.shape[-1])
    part = lax.dot_general(left[:, :rows], own_ref[...], NN, preferred_element_type=F32)
    part += lax.dot_general(left[:, rows:], other_ref[...], NN, preferred_element_type=F32)
    put(part, 0, out_ref, acc_ref)
    finish(at_ref, fix_ref, acc_ref)


def response_kernel(at_ref, left_ref, own_ref, other_ref, out_ref, fix_ref, acc_ref):
    rows, cols = own_ref.shape
    left = left_ref[...].reshape(-1, cols)
    for k, ref in enumerate((own_ref, other_ref)):
        part = lax.dot_general(left, ref[...], NT, preferred_element_type=F32)
        put(part, k * rows, out_ref, acc_ref)
    finish(at_ref, fix_ref, acc_ref)


def sum_kernel(got_ref, fix_ref, out_ref):
    image = total(got_ref, fix_ref).astype(BF16)
    out_ref[...] = jnp.broadcast_to(image[None], out_ref.shape)


def scale_kernel(got_ref, fix_ref, weight_ref, out_ref):
    coef = (total(got_ref, fix_ref) * weight_ref[...]).astype(BF16)
    out_ref[...] = jnp.broadcast_to(coef[None], out_ref.shape)


def final_kernel(got_ref, fix_ref, own_ref, other_ref):
    rows = own_ref.shape[1]
    acc = total(got_ref, fix_ref)
    own_ref[...] = acc[:, :rows]
    other_ref[...] = acc[:, rows:]


def place_kernel(core_ref, own_ref, got_ref, out_ref):
    width = own_ref.shape[0]
    flip = core_ref[0] == 1
    own, got = own_ref[...], got_ref[...]
    out_ref[:width] = jnp.where(flip, got, own)
    out_ref[width:] = jnp.where(flip, own, got)


def weights_kernel(at_ref, mask_hbm, energies_ref, occ_ref, out_ref, mask_ref, mask_t_ref, occ_t_ref, sem):
    lanes = occ_ref.shape[1]
    copy = pltpu.make_async_copy(
        mask_hbm.at[:, pl.ds(pl.multiple_of(at_ref[0] * lanes, lanes), lanes)], mask_ref, sem
    )
    copy.start()
    occ_t_ref[...] = jnp.broadcast_to(occ_ref[pl.ds(at_ref[0], 1), :], (lanes, lanes)).T
    copy.wait()
    mask_t_ref[...] = mask_ref[...].T
    rows = pl.ds(pl.multiple_of(at_ref[1], out_ref.shape[0]), out_ref.shape[0])
    spacing = energies_ref[...] - occ_t_ref[rows, :][:, :1]
    out_ref[...] = jnp.where(mask_t_ref[rows, :] == 1, 1.0 / spacing, 0.0)


def weights(mask, energies, occ, width):
    lanes, cols = 128, mask.shape[0]
    first = lax.axis_index(ROW + ("core",)) * width
    return local(
        weights_kernel,
        [((width, cols), F32)],
        jnp.stack([lax.div(first, lanes), lax.rem(first, lanes)]),
        mask,
        energies.reshape(1, cols),
        occ.reshape(-1, lanes),
        hbm=(1,),
        scratch=(
            pltpu.VMEM((cols, lanes), mask.dtype),
            pltpu.VMEM((lanes, cols), mask.dtype),
            pltpu.VMEM((lanes, lanes), F32),
            pltpu.SemaphoreType.DMA,
        ),
    )[0]


def steps(perturbation, basis, orbitals, pair_mask, energies, occ_energies):
    swap = [(0, 1), (1, 0)]
    core = lax.axis_index("core")
    rows, cols = perturbation.shape
    width = orbitals.shape[1]
    n_row, n_col = lax.axis_size(ROW), lax.axis_size(COL)
    share = width * n_row // n_col
    pert_other = lax.ppermute(perturbation, "core", swap)
    basis_other = lax.ppermute(basis, "core", swap)
    weight = weights(pair_mask, energies, occ_energies, width)
    orbs = exchange(jnp.broadcast_to(orbitals.T[None], (n_row, width, cols)), ROW)
    at_col, at_row = lax.axis_index(COL).reshape(1), lax.axis_index(ROW).reshape(1)
    orbs, pert_other, basis_other, weight, at_col, at_row, core = lax.optimization_barrier(
        (orbs, pert_other, basis_other, weight, at_col, at_row, core.reshape(1))
    )
    n_orb = width * n_row
    by_col = ((n_col, share, 2 * rows), BF16), ((share, 2 * rows), F32)
    by_row = ((n_row, width, cols), BF16), ((width, cols), F32)
    acc_col, acc_row = pltpu.VMEM((n_orb, 2 * rows), F32), pltpu.VMEM((n_orb, cols), F32)
    part, fix = local(
        image_kernel,
        by_col,
        at_col,
        orbs,
        perturbation,
        pert_other,
        hbm=(3,),
        scratch=(acc_col, pltpu.VMEM((2, rows // 2, cols), BF16), pltpu.SemaphoreType.DMA((2,))),
    )
    (image,) = local(sum_kernel, by_col[:1], exchange(part, COL), fix)
    image = exchange(image, COL)
    part, fix = local(
        projection_kernel, by_row, at_row, image, basis, basis_other, scratch=(acc_row,)
    )
    (coef,) = local(scale_kernel, by_row[:1], exchange(part, ROW), fix, weight)
    coef = exchange(coef, ROW)
    part, fix = local(response_kernel, by_col, at_col, coef, basis, basis_other, scratch=(acc_col,))
    own, other = local(final_kernel, [((share, rows), F32)] * 2, exchange(part, COL), fix)
    got = lax.ppermute(other, "core", swap)
    (out,) = local(place_kernel, [((2 * share, rows), F32)], core, own, got)
    return out.T


def solution(mesh):
    sizes = (mesh.shape["row"] // 4, 2, 2, 2, mesh.shape["col"] // 2)
    fine = Mesh(mesh.devices.reshape(sizes), ("y", "xh", "core", "xl", "z"))
    row, col = ("y", "xh", "core"), ("xl", "z")
    return jax.shard_map(
        steps,
        mesh=fine,
        in_specs=(P(row, col), P(row, col), P(col, row), P(col, None), P(col), P()),
        out_specs=P(row, col),
        check_vma=False,
    )
```
